32 devices in a mesh: dp: 4 (over y, core), row: 2 (over x), col: 4 (over z).
Axes of the slice: x: 2, y: 2, z: 4, core: 2. Of those that a mesh axis runs over, the one named last changes fastest.
Arguments:
- tokens: bfloat16 [2048, 1024], P(('dp', 'row'), 'col'), may hold values from -6 to 6
- segment_index: int32 [4, 512], P('dp'), may hold values from 0 to 1, as said below
- cotangent: bfloat16 [2048, 1024], P(('dp', 'row'), 'col'), may hold values from -6 to 6
- norm_gain: float32 [2, 1024], P(None, 'col'), may hold values from 0.25 to 1.75
- gate_weight: bfloat16 [2, 1024, 2048], P(None, 'row', 'col'), may hold values from -0.1875 to 0.1875
- inner_weight: bfloat16 [2, 1024, 2048], P(None, 'row', 'col'), may hold values from -0.1875 to 0.1875
- state_weight: bfloat16 [2, 1024, 256], P(None, 'row'), may hold values from -0.1875 to 0.1875
- step_weight: bfloat16 [2, 1024, 32], P(None, 'row', 'col'), may hold values from -0.1875 to 0.1875
- inner_kernel: float32 [2, 2048, 4], P(None, 'col'), may hold values from -3 to 3
- inner_bias: float32 [2, 2048], P(None, 'col'), may hold values from -0.5 to 0.5
- state_kernel: float32 [2, 256, 4], replicated, may hold values from -3 to 3
- state_bias: float32 [2, 256], replicated, may hold values from -0.5 to 0.5
- step_bias: float32 [2, 32], P(None, 'col'), may hold values from -4 to -1
- decay_log: float32 [2, 32], P(None, 'col'), may hold values from -6.5 to 0.5
- skip_gain: float32 [2, 32], P(None, 'col'), may hold values from 0.5 to 1.5
- gated_gain: float32 [2, 2048], P(None, 'col'), may hold values from 0.25 to 1.75
- output_weight: bfloat16 [2, 2048, 1024], P(None, 'col', 'row'), may hold values from -0.125 to 0.125
Outputs:
- layer_output: bfloat16 [2048, 1024], P(('dp', 'row'), 'col')
- input_grad: float32 [2048, 1024], P(('dp', 'row'), 'col')
- norm_gain_grad: float32 [2, 1024], P(None, 'col')
- gate_weight_grad: float32 [2, 1024, 2048], P(None, ('dp', 'row'), 'col')
- inner_weight_grad: float32 [2, 1024, 2048], P(None, ('dp', 'row'), 'col')
- state_weight_grad: float32 [2, 1024, 256], P(None, ('dp', 'row'), 'col')
- step_weight_grad: float32 [2, 1024, 32], P(None, ('dp', 'row'), 'col')
- inner_kernel_grad: float32 [2, 2048, 4], P(None, 'col')
- inner_bias_grad: float32 [2, 2048], P(None, 'col')
- state_kernel_grad: float32 [2, 256, 4], P(None, 'col')
- state_bias_grad: float32 [2, 256], P(None, 'col')
- step_bias_grad: float32 [2, 32], P(None, 'col')
- decay_log_grad: float32 [2, 32], P(None, 'col')
- skip_gain_grad: float32 [2, 32], P(None, 'col')
- gated_gain_grad: float32 [2, 2048], P(None, 'col')
- output_weight_grad: float32 [2, 2048, 1024], P(None, 'col', ('dp', 'row'))
The draws below stay inside these ranges and needn't reach their ends.
Inputs may be any that keep to these rules, and one draw needn't show every extreme that they name: `segment_index`: each row is one group of 512 tokens holding two sequences: 0 up to a boundary, 1 from it on; each sequence has at least 2048 tokens, or a quarter of 512 where that is fewer.
All inputs are finite; a program needn't handle non-finite values.
Results may differ from the reference program's by a relative error of at most 0.0085.
The reference program's roundings to bfloat16 on the way count: a program that leaves them out, or rounds other values in their place, can miss the bound.
Values may be sent and summed in bfloat16 or wider, within the bound.
A program may use at most 128 MiB of HBM per device.

```python
import jax
import jax.numpy as jnp
from jax import lax

D = 1024
INNER = 2048
HEADS = 32
HEAD_DIM = 64
STATE = 128
KERNEL = 4
SPAN = 256
LAYERS = 2
SEQ_MIN = 2048
TOK_GROUP = 512
GROUPS = 4
TOKENS = 2048


def draw_segment_index(key, part):
    lowest = min(SEQ_MIN, TOK_GROUP // 4)
    cuts = jax.random.randint(key, (GROUPS, 1), lowest, TOK_GROUP - lowest + 1)
    places = jnp.arange(TOK_GROUP, dtype=jnp.int32)[None, :]
    return (places >= cuts).astype(jnp.int32)


def block_levels(own_key, shape, split, smallest, top_value):
    factor_of, own = 1.0, jax.random.fold_in(own_key, 6)
    for dim, blocks in split:
        steps = jnp.exp(jax.random.uniform(jax.random.fold_in(own, dim), (blocks,), jnp.float32, smallest / len(split), top_value / len(split)))
        factor_of = factor_of * jnp.repeat(steps, shape[dim] // blocks).reshape([-1 if axis == dim else 1 for axis in range(len(shape))])
    return factor_of


def scatter_about(key, shape, scale, reach, cuts=(), kind=jnp.bfloat16):
    values = scale * jax.random.normal(key, shape, jnp.float32)
    if cuts:
        values = values * block_levels(key, shape, cuts, -0.22, 0.18)
    return jnp.clip(values, -reach, reach).astype(kind)


def setup_inputs(seed: int = 0) -> dict:
    splits = jax.random.split(jax.random.key(seed), 18)
    return {
        "tokens": scatter_about(splits[0], (TOKENS, D), 1.0, 6.0, ((0, 8), (1, 4))),
        "segment_index": draw_segment_index(jax.random.fold_in(splits[17], 71), 0),
        "cotangent": scatter_about(splits[2], (TOKENS, D), 1.0, 6.0, ((0, 8), (1, 4))),
        "norm_gain": jnp.clip(1.0 + 0.15 * jax.random.normal(splits[3], (LAYERS, D), jnp.float32), 0.25, 1.75),
        "gate_weight": scatter_about(splits[4], (LAYERS, D, INNER), D ** -0.5, 0.1875, ((1, 2), (2, 4))),
        "inner_weight": scatter_about(splits[5], (LAYERS, D, INNER), D ** -0.5, 0.1875, ((1, 2), (2, 4))),
        "state_weight": scatter_about(splits[6], (LAYERS, D, 2 * STATE), D ** -0.5, 0.1875, ((1, 2),)),
        "step_weight": scatter_about(splits[7], (LAYERS, D, HEADS), D ** -0.5, 0.1875, ((1, 2), (2, 4))),
        "inner_kernel": scatter_about(splits[8], (LAYERS, INNER, KERNEL), KERNEL ** -0.5, 3.0, ((1, 4),), jnp.float32),
        "inner_bias": jnp.clip(jax.random.uniform(splits[9], (LAYERS, INNER), jnp.float32, -0.5, 0.5) * block_levels(splits[9], (LAYERS, INNER), ((1, 4),), -0.4, 0.0), -0.5, 0.5),
        "state_kernel": scatter_about(splits[10], (LAYERS, 2 * STATE, KERNEL), KERNEL ** -0.5, 3.0, (), jnp.float32),
        "state_bias": jnp.clip(jax.random.uniform(splits[11], (LAYERS, 2 * STATE), jnp.float32, -0.5, 0.5), -0.5, 0.5),
        "step_bias": jnp.clip(-4.0 + 3.0 * jax.random.uniform(splits[12], (LAYERS, HEADS), jnp.float32) ** block_levels(splits[12], (LAYERS, HEADS), ((1, 4),), -0.2, 0.2), -4.0, -1.0),
        "decay_log": jnp.clip(-6.5 + 7.0 * jax.random.uniform(splits[13], (LAYERS, HEADS), jnp.float32) ** block_levels(splits[13], (LAYERS, HEADS), ((1, 4),), -0.2, 0.2), -6.5, 0.5),
        "skip_gain": jnp.clip(0.5 + 1.0 * jax.random.uniform(splits[14], (LAYERS, HEADS), jnp.float32) ** block_levels(splits[14], (LAYERS, HEADS), ((1, 4),), -0.2, 0.2), 0.5, 1.5),
        "gated_gain": jnp.clip(1.0 + 0.15 * jax.random.normal(splits[15], (LAYERS, INNER), jnp.float32), 0.25, 1.75),
        "output_weight": scatter_about(splits[16], (LAYERS, INNER, D), INNER ** -0.5, 0.125, ((1, 4), (2, 2))),
    }


EPSILON = 1e-05
HIGHEST = lax.Precision.HIGHEST

@jax.custom_vjp
def low(v):
    return lax.optimization_barrier(v.astype(jnp.bfloat16)).astype(jnp.float32)

@jax.custom_vjp
def low_back(v):
    return v

def low_keep(v):
    return (low(v), None)

def low_pass(kept, grad):
    return (grad,)

def back_keep(v):
    return (v, None)

def back_low(kept, grad):
    return (low(grad),)
low.defvjp(low_keep, low_pass)
low_back.defvjp(back_keep, back_low)

def matmul(lhs_mat, rhs_mat):
    return jnp.dot(lhs_mat, rhs_mat, precision=HIGHEST, preferred_element_type=jnp.float32)

def rms_scale(values, gain_row):
    return values * lax.rsqrt(lax.optimization_barrier(jnp.mean(values * values, axis=-1, keepdims=True)) + EPSILON) * gain_row

def causal_conv(values, kernel, bias_row, segments):
    tok_count = values.shape[0]
    padded = jnp.concatenate([jnp.zeros((KERNEL - 1, values.shape[1]), jnp.float32), values], axis=0)
    seg_pad = jnp.concatenate([jnp.full((KERNEL - 1,), -1, jnp.int32), segments.astype(jnp.int32)])
    summed = jnp.zeros_like(values) + bias_row[None, :]
    for offset in range(KERNEL):
        same_seq = (seg_pad[offset:offset + tok_count] == segments).astype(jnp.float32)
        summed = summed + kernel[:, offset][None, :] * padded[offset:offset + tok_count] * same_seq[:, None]
    return jax.nn.silu(summed)

def block_step(state_now, pieces):
    xs_block, dt_block, decay_block, b_block, c_block, seg_block, seg_prior = pieces
    cumulative = jnp.cumsum(decay_block, axis=0)
    places = jnp.arange(SPAN)
    same_seq = (seg_block[:, None] == seg_block[None, :]) & (places[:, None] >= places[None, :])
    spread = cumulative[:, None, :] - cumulative[None, :, :]
    mixing = jnp.exp(jnp.where(same_seq[:, :, None], spread, -60.0)) * same_seq[:, :, None].astype(jnp.float32)
    scores = jnp.dot(c_block, b_block.T, precision=HIGHEST)
    weights = mixing * scores[:, :, None] * dt_block[None, :, :]
    intra_part = jnp.einsum('ijh,jhp->ihp', weights, xs_block, precision=HIGHEST)
    entry_gate = jnp.exp(cumulative) * (seg_block == seg_prior).astype(jnp.float32)[:, None]
    incoming = jnp.einsum('hpn,in->ihp', state_now, c_block, precision=HIGHEST)
    tail_gate = jnp.exp(cumulative[-1][None, :] - cumulative) * (seg_block == seg_block[-1]).astype(jnp.float32)[:, None] * dt_block
    block_decay = jnp.exp(cumulative[-1]) * (seg_block[-1] == seg_prior).astype(jnp.float32)
    fresh_state = jnp.einsum('jh,jhp,jn->hpn', tail_gate, xs_block, b_block, precision=HIGHEST)
    new_state = block_decay[:, None, None] * state_now + fresh_state
    return (new_state, intra_part + entry_gate[:, :, None] * incoming)

def mixer_layer(resid, segments, layer_params):
    norm_gain, gate_weight, inner_weight, state_weight, step_weight, inner_kernel, inner_bias, state_kernel, state_bias, step_bias, decay_log, skip_gain, gated_gain, output_weight = layer_params
    tok_count = resid.shape[0]
    block_count = tok_count // SPAN
    normed = low(rms_scale(resid, norm_gain))
    gate_val = low_back(matmul(normed, gate_weight))
    inner_val = low_back(matmul(normed, inner_weight))
    pair_val = low_back(matmul(normed, state_weight))
    raw_step = low_back(matmul(normed, step_weight))
    xs_all = causal_conv(inner_val, inner_kernel, inner_bias, segments).reshape(tok_count, HEADS, HEAD_DIM)
    pair_post = causal_conv(pair_val, state_kernel, state_bias, segments)
    b_all = pair_post[:, :STATE]
    c_all = pair_post[:, STATE:]
    step_size = jax.nn.softplus(raw_step + step_bias[None, :])
    decay_now = -jnp.exp(decay_log)[None, :] * step_size
    seg_prior = jnp.concatenate([jnp.full((1,), -1, jnp.int32), segments[SPAN - 1:-1:SPAN]])

    def shape_blocks(values):
        return values.reshape((block_count, SPAN) + values.shape[1:])
    start_state = jnp.zeros((HEADS, HEAD_DIM, STATE), jnp.float32)
    unused, mixed_ssd = lax.scan(jax.checkpoint(block_step), start_state, (shape_blocks(xs_all), shape_blocks(step_size), shape_blocks(decay_now), shape_blocks(b_all), shape_blocks(c_all), shape_blocks(segments), seg_prior))
    ssd_out = mixed_ssd.reshape(tok_count, HEADS, HEAD_DIM) + skip_gain[None, :, None] * xs_all
    gated = ssd_out.reshape(tok_count, INNER) * jax.nn.silu(gate_val)
    normed_y = low(rms_scale(gated, gated_gain))
    branch = low_back(matmul(normed_y, output_weight))
    return resid + branch

def reference(tokens, segment_index, cotangent, norm_gain, gate_weight, inner_weight, state_weight, step_weight, inner_kernel, inner_bias, state_kernel, state_bias, step_bias, decay_log, skip_gain, gated_gain, output_weight):
    params = tuple((param.astype(jnp.float32) for param in (norm_gain, gate_weight, inner_weight, state_weight, step_weight, inner_kernel, inner_bias, state_kernel, state_bias, step_bias, decay_log, skip_gain, gated_gain, output_weight)))
    inputs = tokens.astype(jnp.float32).reshape(GROUPS, TOK_GROUP, D)
    cot_all = cotangent.astype(jnp.float32).reshape(GROUPS, TOK_GROUP, D)

    def one_group(totals, element):
        group_in, group_seg, group_cot = element

        def forward(start_val, weights):
            resid = start_val
            for layer_at in range(LAYERS):
                resid = mixer_layer(resid, group_seg, tuple((w_all[layer_at] for w_all in weights)))
            return resid
        result, pullback = jax.vjp(forward, group_in, params)
        grad_in, grad_params = pullback(group_cot)
        totals = tuple((old_sum + new_term for old_sum, new_term in zip(totals, grad_params)))
        return (totals, (result, grad_in))
    zeros_all = tuple((jnp.zeros_like(param) for param in params))
    grads, outputs = lax.scan(one_group, zeros_all, (inputs, segment_index, cot_all))
    layer_output = outputs[0].reshape(TOKENS, D).astype(jnp.bfloat16)
    input_grad = outputs[1].reshape(TOKENS, D)
    return (layer_output, input_grad, grads[0], grads[1], grads[2], grads[3], grads[4], grads[5], grads[6], grads[7], grads[8], grads[9], grads[10], grads[11], grads[12], grads[13])
```

```python
import functools
import types

import jax
import jax.numpy as jnp
from jax import lax
from jax.experimental import pallas as pl
from jax.experimental.pallas import tpu as pltpu
from jax.sharding import PartitionSpec as P

KERNEL = 4
SPAN = 256
LAYERS = 2


EPSILON = 1e-05
HIGHEST = lax.Precision.HIGHEST


def passed_along(value, axis, by):
    devices = lax.axis_size(axis)
    pairs = [(i, i + by) for i in range(devices) if 0 <= i + by < devices]
    return lax.ppermute(value, axis, pairs)


def carried_in(part, axis, combine, identity, reverse):
    count = lax.axis_size(axis)
    place = lax.axis_index(axis)
    if count == 2:
        moved = lax.ppermute(part[1], axis, [(1, 0)] if reverse else [(0, 1)])
        return (None, moved)
    ahead = count - 1 - place if reverse else place
    gathered = jax.tree.map(lambda a: lax.all_gather(a, axis), part)
    state = jax.tree.map(lambda a, e: jnp.zeros_like(a) + jnp.asarray(e, a.dtype), part, identity)

    def one(turn, state):
        source = count - 1 - turn if reverse else turn
        return combine(
            state, jax.tree.map(lambda a: lax.dynamic_index_in_dim(a, source, 0, False), gathered)
        )

    return lax.fori_loop(0, ahead, one, state)


MESH = pl.DeviceIdType.MESH
VMEM_SPEC = pl.BlockSpec(memory_space=pltpu.VMEM)


def greet(peers):
    barrier = pltpu.get_barrier_semaphore()
    for peer in peers:
        pl.semaphore_signal(barrier, inc=1, device_id=peer, device_id_type=MESH)
    pl.semaphore_wait(barrier, len(peers))


def col_peers(n):
    me = lax.axis_index("col")
    return [{"col": lax.rem(me + k, n)} for k in range(1, n)]


def start_to(peers, src_of, dst, send, recv):
    copies = []
    for k, peer in enumerate(peers):
        copy = pltpu.make_async_remote_copy(
            src_ref=src_of(peer),
            dst_ref=dst,
            send_sem=send.at[k],
            recv_sem=recv.at[k],
            device_id=peer,
            device_id_type=MESH,
        )
        copy.start()
        copies.append(copy)
    return copies


def row_sum_kernel(n, value_ref, total_ref, slots, send, recv):
    me = lax.axis_index("col")
    peers = col_peers(n)
    slots[me] = value_ref[...]
    greet(peers)
    copies = start_to(peers, lambda peer: value_ref, slots.at[me], send, recv)
    for copy in copies:
        copy.wait()
    total = slots[0]
    for k in range(1, n):
        total = total + slots[k]
    total_ref[...] = total


def row_total(values):
    n = lax.axis_size("col")
    return pl.pallas_call(
        functools.partial(row_sum_kernel, n),
        out_shape=jax.ShapeDtypeStruct(values.shape, jnp.float32),
        in_specs=[VMEM_SPEC],
        out_specs=VMEM_SPEC,
        scratch_shapes=[
            pltpu.VMEM((n,) + values.shape, jnp.float32),
            pltpu.SemaphoreType.DMA((n - 1,)),
            pltpu.SemaphoreType.DMA((n - 1,)),
        ],
        compiler_params=pltpu.CompilerParams(
            collective_id=0 if values.shape[0] == 1 else 6, has_side_effects=True
        ),
        name="row_total",
    )(values)


def scatter_sum(n, part_ref, outgoing, arrived, send, recv):
    me = lax.axis_index("col")
    peers = col_peers(n)
    width = outgoing.shape[2]
    for k in range(n):
        outgoing[k] = part_ref[:, k * width : (k + 1) * width].astype(outgoing.dtype)
    greet(peers)
    copies = start_to(peers, lambda peer: outgoing.at[peer["col"]], arrived.at[me], send, recv)
    total = part_ref[:, pl.ds(pl.multiple_of(me * width, width), width)]
    for copy in copies:
        copy.wait()
    for peer in peers:
        total = total + arrived[peer["col"]].astype(jnp.float32)
    return total


def share_kernel_sum(n, part_ref, total_ref, arrived, send, recv):
    me = lax.axis_index("col")
    peers = col_peers(n)
    size = total_ref.shape[0]

    def share(at):
        return pl.ds(pl.multiple_of(at * size, size), size)

    greet(peers)
    copies = start_to(
        peers, lambda peer: part_ref.at[share(peer["col"])], arrived.at[me], send, recv
    )
    arrived[me] = part_ref[share(me), :]
    for copy in copies:
        copy.wait()
    total = arrived[0]
    for k in range(1, n):
        total = total + arrived[k]
    total_ref[...] = total


def share_sum(part):
    n = lax.axis_size("col")
    shape = (part.shape[0] // n, part.shape[1])
    return pl.pallas_call(
        functools.partial(share_kernel_sum, n),
        out_shape=jax.ShapeDtypeStruct(shape, jnp.float32),
        in_specs=[VMEM_SPEC],
        out_specs=VMEM_SPEC,
        scratch_shapes=[
            pltpu.VMEM((n,) + shape, jnp.float32),
            pltpu.SemaphoreType.DMA((n - 1,)),
            pltpu.SemaphoreType.DMA((n - 1,)),
        ],
        compiler_params=pltpu.CompilerParams(collective_id=8, has_side_effects=True),
        name="share_sum",
    )(part)


def rows_over_col(n, product, row_own, row_slots, send, recv):
    me = lax.axis_index("col")
    peers = col_peers(n)
    ones = jnp.ones((8, product.shape[1]), jnp.float32)
    sums = lax.dot_general(
        ones, product, (((1,), (1,)), ((), ())), precision=HIGHEST,
        preferred_element_type=jnp.float32,
    )
    row_own[...] = sums
    row_slots[me] = sums
    copies = start_to(peers, lambda peer: row_own, row_slots.at[me], send, recv)
    for copy in copies:
        copy.wait()
    total = row_slots[0]
    for k in range(1, n):
        total = total + row_slots[k]
    return jnp.transpose(total)[:, :1]


def gather_cols(n, own, all_ref, send, recv):
    me = lax.axis_index("col")
    peers = col_peers(n)
    width = own.shape[1]
    place = all_ref.at[:, pl.ds(pl.multiple_of(me * width, width), width)]
    place[...] = own[...]
    copies = start_to(peers, lambda peer: own, place, send, recv)
    for copy in copies:
        copy.wait()


def forward_turn_kernel(
    n, part_ref, resid_ref, gain_ref, resid_out, scale_out, normed_out,
    outgoing, arrived, row_own, row_slots, own, *sems,
):
    resid = resid_ref[...] + scatter_sum(n, part_ref, outgoing, arrived, sems[0], sems[1])
    resid_out[...] = resid
    square = rows_over_col(n, resid * resid, row_own, row_slots, sems[2], sems[3])
    scale = lax.rsqrt(square / (n * resid.shape[1]) + EPSILON)
    scale_out[...] = scale
    own[...] = (resid * scale * gain_ref[...]).astype(jnp.bfloat16)
    gather_cols(n, own, normed_out, sems[4], sems[5])


def backward_turn_kernel(
    n, spread, part_ref, grad_ref, resid_ref, scale_ref, gain_ref, grad_out, gain_out, *rest
):
    if spread:
        cot_out, rest = rest[0], rest[1:]
    outgoing, arrived, row_own, row_slots, own = rest[:5]
    sems = rest[5:]
    d_normed = scatter_sum(n, part_ref, outgoing, arrived, sems[0], sems[1])
    resid = resid_ref[...]
    scale = scale_ref[...]
    scaled_in = d_normed * gain_ref[...]
    gain_out[...] = jnp.sum(d_normed * resid * scale, axis=0, keepdims=True)
    total = rows_over_col(n, scaled_in * resid, row_own, row_slots, sems[2], sems[3])
    grad = (
        grad_ref[...]
        + scale * scaled_in
        - resid * (scale * scale * scale * total / (n * resid.shape[1]))
    )
    grad_out[...] = grad
    if spread:
        own[...] = grad.astype(jnp.bfloat16)
        gather_cols(n, own, cot_out, sems[4], sems[5])


def turn_scratch(n, rows, width):
    return [
        pltpu.VMEM((n, rows, width), jnp.bfloat16),
        pltpu.VMEM((n, rows, width), jnp.bfloat16),
        pltpu.VMEM((8, rows), jnp.float32),
        pltpu.VMEM((n, 8, rows), jnp.float32),
        pltpu.VMEM((rows, width), jnp.bfloat16),
    ] + [pltpu.SemaphoreType.DMA((n - 1,)) for _ in range(6)]


def forward_turn(part, resid, gain):
    n = lax.axis_size("col")
    rows, width = resid.shape
    return pl.pallas_call(
        functools.partial(forward_turn_kernel, n),
        out_shape=[
            jax.ShapeDtypeStruct((rows, width), jnp.float32),
            jax.ShapeDtypeStruct((rows, 1), jnp.float32),
            jax.ShapeDtypeStruct((rows, n * width), jnp.bfloat16),
        ],
        in_specs=[VMEM_SPEC] * 3,
        out_specs=[VMEM_SPEC] * 3,
        scratch_shapes=turn_scratch(n, rows, width),
        compiler_params=pltpu.CompilerParams(collective_id=1, has_side_effects=True),
        name="forward_turn",
    )(part, resid, gain[None, :])


def backward_turn(part, grad, resid, scale, gain, spread):
    n = lax.axis_size("col")
    rows, width = resid.shape
    outs = [
        jax.ShapeDtypeStruct((rows, width), jnp.float32),
        jax.ShapeDtypeStruct((1, width), jnp.float32),
    ]
    if spread:
        outs.append(jax.ShapeDtypeStruct((rows, n * width), jnp.bfloat16))
    return pl.pallas_call(
        functools.partial(backward_turn_kernel, n, spread),
        out_shape=outs,
        in_specs=[VMEM_SPEC] * 5,
        out_specs=[VMEM_SPEC] * len(outs),
        scratch_shapes=turn_scratch(n, rows, width),
        compiler_params=pltpu.CompilerParams(
            collective_id=2 if spread else 3, has_side_effects=True
        ),
        name="backward_turn" if spread else "backward_end",
    )(part, grad, resid, scale[:, None], gain[None, :])


def entry_kernel(n, tok_ref, gain_ref, tok_all, gain_all, *sems):
    me = lax.axis_index("col")
    peers = col_peers(n)
    width = tok_ref.shape[1]
    place = tok_all.at[:, pl.ds(pl.multiple_of(me * width, width), width)]
    place[...] = tok_ref[...]
    gain_all[me] = gain_ref[...]
    greet(peers)
    copies = start_to(peers, lambda peer: tok_ref, place, sems[0], sems[1])
    copies += start_to(peers, lambda peer: gain_ref, gain_all.at[me], sems[2], sems[3])
    for copy in copies:
        copy.wait()


def entry_gather(tokens, gain):
    n = lax.axis_size("col")
    rows, width = tokens.shape
    return pl.pallas_call(
        functools.partial(entry_kernel, n),
        out_shape=[
            jax.ShapeDtypeStruct((rows, n * width), tokens.dtype),
            jax.ShapeDtypeStruct((n, 1, width), gain.dtype),
        ],
        in_specs=[VMEM_SPEC] * 2,
        out_specs=[VMEM_SPEC] * 2,
        scratch_shapes=[pltpu.SemaphoreType.DMA((n - 1,)) for _ in range(4)],
        compiler_params=pltpu.CompilerParams(collective_id=4, has_side_effects=True),
        name="entry_gather",
    )(tokens, gain[None, :])


def start_pair(src, dst, sems, at, peer):
    copy = pltpu.make_async_remote_copy(
        src_ref=src,
        dst_ref=dst,
        send_sem=sems[0].at[at],
        recv_sem=sems[1].at[at],
        device_id=peer,
        device_id_type=MESH,
    )
    copy.start()
    return copy


def load_kernel(n, axes, tok_ref, cot_ref, gain_ref, *rest):
    count = len(axes)
    weights, rest = rest[:count], rest[count:]
    tok_all, cot_all, gain_all = rest[:3]
    wholes, rest = rest[3 : 3 + count * LAYERS], rest[3 + count * LAYERS :]
    col_sems, across, beside, here = rest[:6], rest[6:8], rest[8:10], rest[10]
    me, at_row, at_dp = lax.axis_index("col"), lax.axis_index("row"), lax.axis_index("dp")
    core = lax.rem(at_dp, 2)
    peers = col_peers(n)
    over = {"row": 1 - at_row}
    twin = {"dp": at_dp + 1 - 2 * core}
    width = tok_ref.shape[1]
    columns = pl.ds(pl.multiple_of(me * width, width), width)
    tok_place, cot_place = tok_all.at[:, columns], cot_all.at[:, columns]
    tok_place[...] = tok_ref[...]
    cot_place[...] = cot_ref[...]
    gain_all[me] = gain_ref[...]
    greet(peers + [over, twin])

    def part(ref, axis, start, size):
        window = pl.ds(pl.multiple_of(start, size), size)
        return ref.at[window] if axis == 0 else ref.at[:, window]

    copies = start_to(peers, lambda peer: tok_ref, tok_place, col_sems[0], col_sems[1])
    copies += start_to(peers, lambda peer: gain_ref, gain_all.at[me], col_sems[2], col_sems[3])
    jobs = []
    for layer_at in range(LAYERS):
        for slot, axis in enumerate(axes):
            at = layer_at * count + slot
            block, whole = weights[slot].at[layer_at], wholes[at]
            size = block.shape[axis]
            half = size // 2
            sent = start_pair(
                part(block, axis, core * half, half),
                part(whole, axis, at_row * size + core * half, half),
                across,
                at,
                over,
            )
            kept = pltpu.make_async_copy(
                block, part(whole, axis, at_row * size, size), here.at[at]
            )
            kept.start()
            jobs.append((sent, kept, whole, axis, size, half))
    copies += start_to(peers, lambda peer: cot_ref, cot_place, col_sems[4], col_sems[5])
    passed = []
    for at, (sent, kept, whole, axis, size, half) in enumerate(jobs):
        sent.wait_recv()
        landed = part(whole, axis, (1 - at_row) * size + core * half, half)
        passed.append(start_pair(landed, landed, beside, at, twin))
    for sent, kept, *unused in jobs:
        sent.wait_send()
        kept.wait()
    for copy in passed + copies:
        copy.wait()


def load_all(tokens, cotangent, gain, weights, axes):
    n = lax.axis_size("col")
    rows, width = tokens.shape
    outs = [
        jax.ShapeDtypeStruct((rows, n * width), tokens.dtype),
        jax.ShapeDtypeStruct((rows, n * width), cotangent.dtype),
        jax.ShapeDtypeStruct((n, 1, width), gain.dtype),
    ]
    for layer_at in range(LAYERS):
        for weight, axis in zip(weights, axes):
            shape = list(weight.shape[1:])
            shape[axis] *= 2
            outs.append(jax.ShapeDtypeStruct(tuple(shape), weight.dtype))
    count = len(weights) * LAYERS
    return pl.pallas_call(
        functools.partial(load_kernel, n, axes),
        out_shape=outs,
        in_specs=[VMEM_SPEC] * (3 + len(weights)),
        out_specs=[VMEM_SPEC] * (3 + count),
        scratch_shapes=[pltpu.SemaphoreType.DMA((n - 1,)) for _ in range(6)]
        + [pltpu.SemaphoreType.DMA((count,)) for _ in range(5)],
        compiler_params=pltpu.CompilerParams(collective_id=7, has_side_effects=True, vmem_limit_bytes=40 * 2**20),
        name="load_all",
    )(tokens, cotangent, gain[None, :], *weights)


def small_kernel(dp, row, value_ref, total_ref, slots, send, recv):
    at_dp, at_row = lax.axis_index("dp"), lax.axis_index("row")
    me = at_dp * row + at_row
    peers = []
    for k in range(1, dp * row):
        peers.append(
            {"dp": lax.rem(at_dp + k // row, dp), "row": lax.rem(at_row + k % row, row)}
        )
    slots[me] = value_ref[...]
    greet(peers)
    copies = start_to(peers, lambda peer: value_ref, slots.at[me], send, recv)
    for copy in copies:
        copy.wait()
    total = slots[0]
    for k in range(1, dp * row):
        total = total + slots[k]
    total_ref[...] = total


def small_total(value):
    dp, row = lax.axis_size("dp"), lax.axis_size("row")
    count = dp * row
    if count > 8:
        return lax.psum(value, ("dp", "row"))
    return pl.pallas_call(
        functools.partial(small_kernel, dp, row),
        out_shape=jax.ShapeDtypeStruct(value.shape, jnp.float32),
        in_specs=[VMEM_SPEC],
        out_specs=VMEM_SPEC,
        scratch_shapes=[
            pltpu.VMEM((count,) + value.shape, jnp.float32),
            pltpu.SemaphoreType.DMA((count - 1,)),
            pltpu.SemaphoreType.DMA((count - 1,)),
        ],
        compiler_params=pltpu.CompilerParams(collective_id=5, has_side_effects=True),
        name="small_total",
    )(value)


def whole_over_row(block, axis):
    if lax.axis_size("row") != 2:
        return lax.all_gather(block, "row", axis=axis, tiled=True)
    other = lax.ppermute(block, "row", [(0, 1), (1, 0)])
    size = block.shape[axis]
    trio = jnp.concatenate([block, other, block], axis=axis)
    return lax.dynamic_slice_in_dim(trio, lax.axis_index("row") * size, 2 * size, axis)


def whole_over_col(block):
    n = lax.axis_size("col")
    size = block.shape[1]
    blocks = [block]
    for k in range(1, n):
        blocks.append(lax.ppermute(block, "col", [(i, (i - k) % n) for i in range(n)]))
    twice = jnp.concatenate(blocks + blocks[:-1], axis=1)
    start = lax.rem(n - lax.axis_index("col"), n) * size
    return lax.dynamic_slice_in_dim(twice, start, n * size, 1)


def packed_small(parts):
    flat = jnp.concatenate([part.reshape(-1) for part in parts])
    total = flat.shape[0]
    lines = -(-total // 1024) * 8
    return jnp.pad(flat, (0, lines * 128 - total)).reshape(lines, 128)


def unpacked_small(packed, shapes):
    flat = packed.reshape(-1)
    out, at = [], 0
    for shape in shapes:
        size = 1
        for extent in shape:
            size *= extent
        out.append(flat[at : at + size].reshape(shape))
        at += size
    return out


def link_up(earlier, later):
    return (earlier[0] * later[0], later[0][:, None, None] * earlier[1] + later[1])


def link_down(earlier, later):
    return (earlier[0] * later[0], later[1] + later[0][:, None, None] * earlier[1])


def mixer_parts(
    post_x, b_mat, c_mat, raw_step, step_off, decay_rate, skip_rate, segments, seg_prior
):
    tok_count = post_x.shape[0]
    head_count = raw_step.shape[1]
    head_width = post_x.shape[1] // head_count
    block_count = tok_count // SPAN
    step_size = jax.nn.softplus(raw_step + step_off[None, :])
    decay_now = -jnp.exp(decay_rate)[None, :] * step_size
    xs_c = post_x.reshape(block_count, SPAN, head_count, head_width)
    step_c = step_size.reshape(block_count, SPAN, head_count)
    ordered = jnp.arange(SPAN)
    cumulative = jnp.einsum(
        "ij,cjh->cih",
        (ordered[:, None] >= ordered[None, :]).astype(jnp.float32),
        decay_now.reshape(block_count, SPAN, head_count),
        precision=HIGHEST,
    )
    b_c = b_mat.reshape(block_count, SPAN, -1)
    c_c = c_mat.reshape(block_count, SPAN, -1)
    seg_c = segments.reshape(block_count, SPAN)
    places = jnp.arange(SPAN)
    same_seq = (seg_c[:, :, None] == seg_c[:, None, :]) & (places[:, None] >= places[None, :])[None]
    causal = same_seq.astype(jnp.float32)[:, None, :, :]
    cum_heads = jnp.transpose(cumulative, (0, 2, 1))
    step_heads = jnp.transpose(step_c, (0, 2, 1))
    spread = cum_heads[:, :, :, None] - cum_heads[:, :, None, :]
    scores = jnp.einsum("cin,cjn->cij", c_c, b_c, precision=HIGHEST)
    weights = jnp.exp(spread * causal) * causal * scores[:, None, :, :] * step_heads[:, :, None, :]
    intra_part = jnp.einsum("chij,cjhp->cihp", weights, xs_c, precision=HIGHEST)
    entry_gate = jnp.exp(cumulative) * (seg_c == seg_prior[:, None]).astype(jnp.float32)[..., None]
    tail_gate = (
        jnp.exp(cumulative[:, -1:, :] - cumulative)
        * (seg_c == seg_c[:, -1:]).astype(jnp.float32)[..., None]
        * step_c
    )
    fresh_state = jnp.einsum("cjh,cjhp,cjn->chpn", tail_gate, xs_c, b_c, precision=HIGHEST)
    block_decay = (
        jnp.exp(cumulative[:, -1, :]) * (seg_c[:, -1] == seg_prior).astype(jnp.float32)[:, None]
    )

    def advance(state_now, element):
        return (element[1][:, None, None] * state_now + element[0], state_now)

    dev_state, starts = lax.scan(
        advance, jnp.zeros_like(fresh_state[0]), (fresh_state, block_decay)
    )
    prefixes = [jnp.ones_like(block_decay[0])]
    for at in range(block_count - 1):
        prefixes.append(prefixes[-1] * block_decay[at])
    prefix = jnp.stack(prefixes, axis=0)
    dev_decay = prefix[-1] * block_decay[-1]
    local_part = intra_part + skip_rate[None, None, :, None] * xs_c
    return (local_part, entry_gate, c_c, starts, prefix, dev_state, dev_decay)


def mixer_finish(pieces, entry_state):
    local_part, entry_gate, c_c, starts, prefix, dev_state, dev_decay = pieces
    states = starts + prefix[:, :, None, None] * entry_state[None]
    incoming = jnp.einsum("chpn,cin->cihp", states, c_c, precision=HIGHEST)
    mixed_out = local_part + entry_gate[..., None] * incoming
    return mixed_out.reshape(mixed_out.shape[0] * SPAN, -1)


def mixer_core(
    post_x,
    b_mat,
    c_mat,
    raw_step,
    step_off,
    decay_rate,
    skip_rate,
    entry_state,
    segments,
    seg_prior,
):
    pieces = mixer_parts(
        post_x, b_mat, c_mat, raw_step, step_off, decay_rate, skip_rate, segments, seg_prior
    )
    return (mixer_finish(pieces, entry_state), pieces[5], pieces[6])


def local(
    tokens,
    segment_index,
    cotangent,
    norm_gain,
    gate_weight,
    inner_weight,
    state_weight,
    step_weight,
    inner_kernel,
    inner_bias,
    state_kernel,
    state_bias,
    step_bias,
    decay_log,
    skip_gain,
    gated_gain,
    output_weight,
):
    tok_rows = tokens.shape[0]
    full_width = tokens.shape[1] * lax.axis_size("col")
    head_count = step_bias.shape[1]
    inner_cols = inner_kernel.shape[1]
    inner_full = inner_cols * lax.axis_size("col")
    state_cols = state_kernel.shape[1]
    state_half = state_cols // 2
    share_cols = state_cols // lax.axis_size("col")
    col_at = lax.axis_index("col")
    first_tok = lax.axis_index("row") * tok_rows
    group_seg = segment_index[0]
    seg_front = jnp.concatenate([jnp.full((KERNEL - 1,), -1, jnp.int32), group_seg])
    seg_rear = jnp.concatenate([group_seg, jnp.full((KERNEL - 1,), -2, jnp.int32)])
    seg_early = lax.dynamic_slice_in_dim(seg_front, first_tok, tok_rows + KERNEL - 1)
    seg_late = lax.dynamic_slice_in_dim(seg_rear, first_tok, tok_rows + KERNEL - 1)
    segments = seg_early[KERNEL - 1 :]
    seg_prior = jnp.concatenate(
        [seg_early[KERNEL - 2 : KERNEL - 1], segments[SPAN - 1 : -1 : SPAN]]
    )
    dims_t = (((1,), (1,)), ((), ()))
    dims_w = (((0,), (0,)), ((), ()))
    resid = tokens.astype(jnp.float32)
    paired = lax.axis_size("row") == 2 and lax.axis_size("dp") % 2 == 0
    if paired:
        tokens_all, cot_all, gain_all, *wholes = load_all(
            tokens,
            cotangent,
            norm_gain[0],
            (gate_weight, inner_weight, state_weight, output_weight),
            (0, 0, 0, 1),
        )
    else:
        tokens_all, gain_all = entry_gather(tokens, norm_gain[0])
        cot_all = whole_over_col(cotangent)
    first_all = tokens_all.astype(jnp.float32)
    row_scale = lax.rsqrt(jnp.sum(first_all * first_all, axis=1) / full_width + EPSILON)
    normed_all = (first_all * row_scale[:, None] * gain_all.reshape(1, -1)).astype(jnp.bfloat16)
    whole_weights = []
    for layer_at in range(LAYERS):
        step_full = whole_over_row(step_weight[layer_at], 0)
        if paired:
            gate_full, inner_whole, state_full, output_full = wholes[
                4 * layer_at : 4 * layer_at + 4
            ]
        else:
            gate_full = whole_over_row(gate_weight[layer_at], 0)
            inner_whole = whole_over_row(inner_weight[layer_at], 0)
            state_full = whole_over_row(state_weight[layer_at], 0)
            output_full = whole_over_row(output_weight[layer_at], 1)
        whole_weights.append((gate_full, inner_whole, state_full, step_full, output_full))
    saved = []
    for layer_at in range(LAYERS):
        gate_full, inner_whole, state_full, step_full, output_full = whole_weights[layer_at]
        gate_val = jnp.dot(normed_all, gate_full, preferred_element_type=jnp.float32)
        inner_val = jnp.dot(normed_all, inner_whole, preferred_element_type=jnp.float32)
        pair_val = jnp.dot(normed_all, state_full, preferred_element_type=jnp.float32)
        raw_step = jnp.dot(normed_all, step_full, preferred_element_type=jnp.float32)
        values = jnp.concatenate([inner_val, pair_val], axis=1)
        before = passed_along(values[tok_rows - (KERNEL - 1) :], "row", 1)
        padded = jnp.concatenate([before, values], axis=0)
        kernels = jnp.concatenate([inner_kernel[layer_at], state_kernel[layer_at]], axis=0)
        pre_act = (
            jnp.zeros_like(values)
            + jnp.concatenate([inner_bias[layer_at], state_bias[layer_at]])[None, :]
        )
        for offset in range(KERNEL):
            same_seq = (seg_early[offset : offset + tok_rows] == segments).astype(jnp.float32)
            pre_act = (
                pre_act
                + kernels[:, offset][None, :]
                * padded[offset : offset + tok_rows]
                * same_seq[:, None]
            )
        post_act = jax.nn.silu(pre_act)
        post_x = post_act[:, :inner_cols]
        b_mat = post_act[:, inner_cols : inner_cols + state_half]
        c_mat = post_act[:, inner_cols + state_half :]
        pieces = mixer_parts(
            post_x,
            b_mat,
            c_mat,
            raw_step,
            step_bias[layer_at],
            decay_log[layer_at],
            skip_gain[layer_at],
            segments,
            seg_prior,
        )
        unused, entry_state = carried_in(
            (pieces[6], pieces[5]),
            "row",
            link_up,
            (jnp.ones_like(pieces[6]), jnp.zeros_like(pieces[5])),
            False,
        )
        mixed_out = mixer_finish(pieces, entry_state)
        silu_gate = jax.nn.silu(gate_val)
        gated = mixed_out * silu_gate
        power_part = jnp.sum(gated * gated, axis=1)
        if layer_at + 1 < LAYERS:
            power_sum = row_total(power_part[None, :])[0]
        else:
            last_dyn = lax.dot_general(
                cot_all, output_full, dims_t, preferred_element_type=jnp.float32
            )
            last_scaled = last_dyn * gated_gain[layer_at][None, :]
            power_sum, last_total = row_total(
                jnp.stack([power_part, jnp.sum(last_scaled * gated, axis=1)], axis=0)
            )
        gated_scale = lax.rsqrt(power_sum / inner_full + EPSILON)
        normed_y = (gated * gated_scale[:, None] * gated_gain[layer_at][None, :]).astype(
            jnp.bfloat16
        )
        partial_out = jnp.dot(normed_y, output_full, preferred_element_type=jnp.float32)
        stored = None
        saved.append(
            (
                resid,
                row_scale,
                normed_all,
                gate_val,
                padded,
                pre_act,
                post_x,
                b_mat,
                c_mat,
                raw_step,
                entry_state,
                pieces[4],
                pieces[1],
                pieces[6],
                mixed_out,
                silu_gate,
                gated,
                gated_scale,
                normed_y,
                stored,
            )
        )
        if layer_at + 1 < LAYERS:
            resid, new_scale, normed_all = forward_turn(
                partial_out, resid, norm_gain[layer_at + 1]
            )
            row_scale = new_scale[:, 0]
        else:
            resid = resid + lax.psum_scatter(partial_out, "col", scatter_dimension=1, tiled=True)
    layer_output = resid.astype(jnp.bfloat16)
    resid_grad = cotangent.astype(jnp.float32)
    big_grads = [None] * LAYERS
    small_terms = [None] * LAYERS
    for layer_at in reversed(range(LAYERS)):
        (
            resid,
            row_scale,
            normed_all,
            gate_val,
            padded,
            pre_act,
            post_x,
            b_mat,
            c_mat,
            raw_step,
            entry_state,
            prefix,
            entry_gate,
            dev_decay,
            mixed_out,
            silu_gate,
            gated,
            gated_scale,
            normed_y,
            stored,
        ) = saved[layer_at]
        gate_full, inner_whole, state_full, step_full, output_full = whole_weights[layer_at]
        if layer_at + 1 < LAYERS:
            d_normed_y = lax.dot_general(
                cot_all, output_full, dims_t, preferred_element_type=jnp.float32
            )
        else:
            d_normed_y = last_dyn
        grad_out = lax.dot_general(cot_all, normed_y, dims_w, preferred_element_type=jnp.float32)
        scaled_y = d_normed_y * gated_gain[layer_at][None, :]
        if layer_at + 1 < LAYERS:
            total_y = row_total(jnp.sum(scaled_y * gated, axis=1)[None, :])[0]
        else:
            total_y = last_total
        d_gated = (
            gated_scale[:, None] * scaled_y
            - gated * (gated_scale**3 * total_y / inner_full)[:, None]
        )
        gain_y = jnp.sum(d_normed_y * gated * gated_scale[:, None], axis=0)
        d_mixed = d_gated * silu_gate
        sigma_gate = jax.nn.sigmoid(gate_val)
        d_gate = d_gated * mixed_out * sigma_gate * (1.0 + gate_val * (1.0 - sigma_gate))
        block_count = tok_rows // SPAN
        d_mixed_c = d_mixed.reshape(block_count, SPAN, head_count, -1)
        c_blocks = c_mat.reshape(block_count, SPAN, -1)
        reach_gate = prefix[:, None, :] * entry_gate
        local_pull = jnp.einsum(
            "cih,cihp,cin->hpn", reach_gate, d_mixed_c, c_blocks, precision=HIGHEST
        )
        unused_b, state_pull = carried_in(
            (dev_decay, local_pull),
            "row",
            link_down,
            (jnp.ones_like(dev_decay), jnp.zeros_like(local_pull)),
            True,
        )
        decay_pull = jnp.sum(state_pull * entry_state, axis=(1, 2))

        def local_mixer(px_val, bm_val, cm_val, rs_val, so_val, dr_val, sr_val, es_val):
            return mixer_core(
                px_val, bm_val, cm_val, rs_val, so_val, dr_val, sr_val, es_val, segments, seg_prior
            )

        unused_c, pullback = jax.vjp(
            local_mixer,
            post_x,
            b_mat,
            c_mat,
            raw_step,
            step_bias[layer_at],
            decay_log[layer_at],
            skip_gain[layer_at],
            entry_state,
        )
        d_post_x, grad_b, grad_c, d_raw_step, g_step_bias, g_decay, g_skip, unused_d = pullback(
            (d_mixed, state_pull, decay_pull)
        )
        d_share = share_sum(jnp.concatenate([grad_b.T, grad_c.T], axis=0)).T
        d_post = jnp.concatenate([d_post_x, d_share], axis=1)
        share_pre = lax.dynamic_slice_in_dim(
            pre_act[:, inner_cols:], col_at * share_cols, share_cols, 1
        )
        own_pre = jnp.concatenate([pre_act[:, :inner_cols], share_pre], axis=1)
        sigma_pre = jax.nn.sigmoid(own_pre)
        d_pre = d_post * sigma_pre * (1.0 + own_pre * (1.0 - sigma_pre))
        after_rows = passed_along(d_pre[: KERNEL - 1], "row", -1)
        d_pre_ext = jnp.concatenate([d_pre, after_rows], axis=0)
        share_kernel = lax.dynamic_slice_in_dim(
            state_kernel[layer_at], col_at * share_cols, share_cols, 0
        )
        own_kernel = jnp.concatenate([inner_kernel[layer_at], share_kernel], axis=0)
        share_padded = lax.dynamic_slice_in_dim(
            padded[:, inner_cols:], col_at * share_cols, share_cols, 1
        )
        own_padded = jnp.concatenate([padded[:, :inner_cols], share_padded], axis=1)
        d_values = jnp.zeros_like(d_pre)
        kernel_terms = []
        for offset in range(KERNEL):
            lead_by = KERNEL - 1 - offset
            same_back = (seg_late[lead_by : lead_by + tok_rows] == segments).astype(jnp.float32)
            d_values = (
                d_values
                + own_kernel[:, offset][None, :]
                * d_pre_ext[lead_by : lead_by + tok_rows]
                * same_back[:, None]
            )
            same_fwd = (seg_early[offset : offset + tok_rows] == segments).astype(jnp.float32)
            kernel_terms.append(
                jnp.sum(d_pre * own_padded[offset : offset + tok_rows] * same_fwd[:, None], axis=0)
            )
        kernel_grad = jnp.stack(kernel_terms, axis=0)
        bias_grad = jnp.sum(d_pre, axis=0)
        d_gate16 = d_gate.astype(jnp.bfloat16)
        d_inner16 = d_values[:, :inner_cols].astype(jnp.bfloat16)
        d_pair16 = d_values[:, inner_cols:].astype(jnp.bfloat16)
        d_step16 = d_raw_step.astype(jnp.bfloat16)
        share_weight = lax.dynamic_slice_in_dim(state_full, col_at * share_cols, share_cols, 1)
        partial_in = lax.dot_general(
            d_gate16, gate_full, dims_t, preferred_element_type=jnp.float32
        )
        partial_in = partial_in + lax.dot_general(
            d_inner16, inner_whole, dims_t, preferred_element_type=jnp.float32
        )
        partial_in = partial_in + lax.dot_general(
            d_pair16, share_weight, dims_t, preferred_element_type=jnp.float32
        )
        partial_in = partial_in + lax.dot_general(
            d_step16, step_full, dims_t, preferred_element_type=jnp.float32
        )
        low_grads = jnp.concatenate([d_gate16, d_inner16, d_pair16, d_step16], axis=1)
        low_grads = jnp.pad(low_grads, ((0, 0), (0, -low_grads.shape[1] % 128)))
        grad_in = lax.dot_general(normed_all, low_grads, dims_w, preferred_element_type=jnp.float32)
        layer_grads = jnp.concatenate(
            [grad_out.astype(jnp.bfloat16), grad_in.astype(jnp.bfloat16)], axis=1
        )
        if layer_at > 0:
            layer_grads, partial_in = lax.optimization_barrier((layer_grads, partial_in))
        big_grads[layer_at] = lax.psum_scatter(
            layer_grads, ("dp", "row"), scatter_dimension=0, tiled=True
        ).astype(jnp.float32)
        turned = backward_turn(
            partial_in, resid_grad, resid, row_scale, norm_gain[layer_at], layer_at > 0
        )
        resid_grad, gain_in = turned[0], turned[1][0]
        if layer_at > 0:
            cot_all = turned[2]
        small_terms[layer_at] = (
            gain_in,
            gain_y,
            kernel_grad[:, :inner_cols],
            bias_grad[:inner_cols],
            kernel_grad[:, inner_cols:],
            bias_grad[inner_cols:],
            g_step_bias,
            g_decay,
            g_skip,
        )

    model_cols = output_weight.shape[1]
    sizes = (model_cols, inner_cols, inner_cols, share_cols, head_count)
    summed, at = [], 0
    for size in sizes:
        summed.append(jnp.stack([big[:, at : at + size] for big in big_grads], axis=0))
        at += size
    shapes = [part.shape for terms in small_terms for part in terms]
    unpacked = unpacked_small(
        small_total(packed_small([part for terms in small_terms for part in terms])), shapes
    )
    count = len(small_terms[0])
    smalls = [
        jnp.stack([unpacked[layer_at * count + slot] for layer_at in range(LAYERS)], axis=0)
        for slot in range(count)
    ]
    return (
        layer_output,
        resid_grad,
        smalls[0],
        summed[1],
        summed[2],
        summed[3],
        summed[4],
        jnp.swapaxes(smalls[2], 1, 2),
        smalls[3],
        jnp.swapaxes(smalls[4], 1, 2),
        smalls[5],
        smalls[6],
        smalls[7],
        smalls[8],
        smalls[1],
        jnp.transpose(summed[0], (0, 2, 1)),
    )


NN = (((1,), (0,)), ((), ()))
NT = (((1,), (1,)), ((), ()))
TN = (((0,), (0,)), ((), ()))
BF = jnp.bfloat16
F32 = jnp.float32


def mm(a, b, dims=NN):
    return lax.dot_general(a, b, dims, preferred_element_type=F32)


def halves(a):
    high = a.astype(BF)
    return high, (a - high.astype(F32)).astype(BF)


def thirds(a):
    high = a.astype(BF)
    rest = a - high.astype(F32)
    middle = rest.astype(BF)
    return high, middle, (rest - middle.astype(F32)).astype(BF)


def mm_halves(a, b, dims=NN):
    return mm(a[0], b[0], dims) + (mm(a[0], b[1], dims) + mm(a[1], b[0], dims))


def mm3(a, b, dims=NN):
    return mm_halves(halves(a), halves(b), dims)


def selector_times(selector, b, dims=NN):
    high, low = halves(b)
    return mm(selector, high, dims) + mm(selector, low, dims)


def times_selector(a, selector):
    high, middle, low = thirds(a)
    return mm(high, selector) + (mm(middle, selector) + mm(low, selector))


def logistic(v):
    return 1.0 / (1.0 + jnp.exp(-v))


class Links:
    def __init__(self, send, recv):
        self.send, self.recv, self.at = send, recv, 0

    def push(self, src, dst, peer):
        copy = pltpu.make_async_remote_copy(
            src_ref=src,
            dst_ref=dst,
            send_sem=self.send.at[self.at],
            recv_sem=self.recv.at[self.at],
            device_id=peer,
            device_id_type=MESH,
        )
        copy.start()
        self.at += 1
        return copy


def wait_all(copies):
    for copy in copies:
        copy.wait()


def fused_kernel(n, names, *refs):
    r = types.SimpleNamespace(**dict(zip(names, refs)))
    rows, width = r.tok.shape
    full = n * width
    share_rows = rows // n
    cols = r.gate.shape[2]
    heads = cols // 64
    pairs = heads // 2
    state_cols = r.state.shape[2]
    half_state = state_cols // 2
    share = state_cols // n
    deep = r.gate.shape[1]
    me, x, dp = lax.axis_index("col"), lax.axis_index("row"), lax.axis_index("dp")
    core, y = lax.rem(dp, 2), dp // 2
    peers = [
        {"col": lax.rem(me + 2, n)}, {"col": n - 1 - me}, {"col": me + 1 - 2 * lax.rem(me, 2)}
    ]
    over, twin, beside = {"row": 1 - x}, {"dp": dp + 1 - 2 * core}, {"dp": lax.rem(dp + 2, 4)}
    links = Links(r.send, r.recv)
    here = iter(range(64))

    def lanes(at, size):
        return pl.ds(pl.multiple_of(at * size, size), size)

    def bring(src, dst):
        copy = pltpu.make_async_copy(src, dst, r.here.at[next(here)])
        copy.start()
        return copy

    own_copies = [
        bring(r.tok, r.tok_all.at[:, lanes(me, width)]),
        bring(r.cot, r.cot_all.at[:, lanes(me, width)]),
        bring(r.gain, r.gain_all.at[me]),
        bring(r.in_seg, r.seg),
        bring(r.in_taps, r.taps),
        bring(r.in_bias, r.bias),
        bring(r.in_gated, r.gated_gain),
        bring(r.in_pair_taps, r.pair_taps),
        bring(r.in_pair_bias, r.pair_bias),
        bring(r.in_step, r.step_bias),
        bring(r.in_decay, r.decay_log),
        bring(r.in_skip, r.skip_gain),
    ]
    greet(peers + [over, twin, beside])

    def to_cols(src_of, dst):
        return [links.push(src_of(peer["col"]), dst, peer) for peer in peers]

    tok_copies = to_cols(lambda at: r.tok, r.tok_all.at[:, lanes(me, width)])
    tok_copies += to_cols(lambda at: r.gain, r.gain_all.at[me])

    def window(ref, axis, start, size):
        at = pl.ds(pl.multiple_of(start, size), size)
        return ref.at[at] if axis == 0 else ref.at[:, at]

    class Block:
        def __init__(self, source, whole, axis):
            self.source, self.whole, self.axis = source, whole, axis
            self.size = source.shape[axis]
            self.half = self.size // 2

        def begin(self):
            self.kept = bring(
                self.source, window(self.whole, self.axis, x * self.size, self.size)
            )
            where = pl.ds(pl.multiple_of(x * self.size + core * self.half, self.half), self.half)
            target = self.whole.at[where] if self.axis == 0 else self.whole.at[:, where]
            self.sent = links.push(
                window(self.source, self.axis, core * self.half, self.half), target, over
            )
            return self

        def turn(self):
            self.sent.wait_recv()
            where = pl.ds(
                pl.multiple_of((1 - x) * self.size + core * self.half, self.half), self.half
            )
            landed = self.whole.at[where] if self.axis == 0 else self.whole.at[:, where]
            self.passed = links.push(landed, landed, twin)

        def end(self):
            self.sent.wait_send()
            self.kept.wait()
            self.passed.wait()

    def inward(layer):
        return [
            Block(r.inner.at[layer], r.inner_all.at[layer], 0).begin(),
            Block(r.state.at[layer], r.state_all.at[layer], 0).begin(),
            Block(r.step.at[layer], r.step_all.at[layer], 0).begin(),
            Block(r.gate.at[layer], r.gate_all.at[layer], 0).begin(),
        ]

    def outward(layer):
        return Block(r.out.at[layer], r.out_all.at[layer], 1).begin()

    first_in = inward(0)
    first_out = outward(0)

    wait_all(own_copies)
    seg = r.seg[...].astype(F32)
    seg_cols = jnp.transpose(jnp.broadcast_to(seg, (8, 2 * rows)))
    r.segp[0:8, :] = jnp.full((8, 8), -1.0, F32)
    r.segp[8 : 8 + 2 * rows, :] = seg_cols
    r.segp[8 + 2 * rows : 16 + 2 * rows, :] = jnp.full((8, 8), -2.0, F32)

    def seg_at(shift):
        first = r.segp[8 + shift : 8 + shift + rows, :]
        second = r.segp[8 + rows + shift : 8 + rows + shift + rows, :]
        return jnp.where(x == 0, first, second)[:, 0:1]

    def same_at(shift):
        return (seg_at(shift) == seg_at(0)).astype(F32)

    seg_row = jnp.where(x == 0, seg[:, :rows], seg[:, rows:])
    down = lax.broadcasted_iota(jnp.int32, (rows, rows), 0)
    along = lax.broadcasted_iota(jnp.int32, (rows, rows), 1)
    alike = seg_at(0) == seg_row
    r.mask[...] = jnp.where(alike & (down >= along), 0.0, -1e30)
    r.mask_t[...] = jnp.where(alike & (down <= along), 0.0, -1e30)
    r.upper[...] = (down <= along).astype(F32).astype(BF)
    r.lower[...] = (down >= along).astype(F32).astype(BF)
    prior = jnp.where(x == 0, -1.0, seg[:, rows - 1 : rows])
    seg_last = seg_row[:, rows - 1 : rows]
    entry_mask = (seg_row == prior).astype(F32)
    tail_mask = (seg_row == seg_last).astype(F32)
    pass_mask = (seg_last == prior).astype(F32)
    head_of = (
        lax.broadcasted_iota(jnp.int32, (heads, cols), 1) // 64
        == lax.broadcasted_iota(jnp.int32, (heads, cols), 0)
    )
    r.pick[...] = head_of.astype(F32).astype(BF)
    left = lax.broadcasted_iota(jnp.int32, (rows, 128), 1) < 64
    eye = (
        lax.broadcasted_iota(jnp.int32, (heads, heads), 0)
        == lax.broadcasted_iota(jnp.int32, (heads, heads), 1)
    )

    def upright(row):
        return jnp.sum(jnp.where(eye, row, 0.0), axis=1, keepdims=True)

    def flat(column):
        return jnp.sum(jnp.where(eye, column, 0.0), axis=0, keepdims=True)

    for layer in range(LAYERS):
        r.head_par[layer, :, 0:1] = upright(r.step_bias[layer : layer + 1, :])
        r.head_par[layer, :, 1:2] = upright(r.decay_log[layer : layer + 1, :])
        r.skip_row[layer : layer + 1, :] = jnp.sum(
            jnp.where(head_of, upright(r.skip_gain[layer : layer + 1, :]), 0.0),
            axis=0,
            keepdims=True,
        )
    last_lane = lax.broadcasted_iota(jnp.int32, (heads, rows), 1) == rows - 1

    def spread(columns):
        return jnp.concatenate(
            [
                jnp.where(left, columns[:, 2 * p : 2 * p + 1], columns[:, 2 * p + 1 : 2 * p + 2])
                for p in range(pairs)
            ],
            axis=1,
        )

    def per_head(v):
        return selector_times(r.pick[...], v, NT)

    def row_sums(v):
        return selector_times(jnp.ones((8, v.shape[1]), BF), v, NT)

    def col_exchange(slot, values):
        r.sum_own[slot] = values
        r.sum_all[slot, me] = values
        return to_cols(lambda at: r.sum_own.at[slot], r.sum_all.at[slot, me])

    def col_total(slot, copies):
        wait_all(copies)
        total = r.sum_all[slot, 0]
        for k in range(1, n):
            total = total + r.sum_all[slot, k]
        return jnp.transpose(total)

    def own_share(value):
        total = value[:, 0:share]
        for k in range(1, n):
            total = jnp.where(me == k, value[:, k * share : (k + 1) * share], total)
        return total

    def tokens_out(slot, partial, parts=1):
        r.part[...] = partial
        r.rs_out[slot] = partial.astype(BF)
        mine = pl.ds(pl.multiple_of(me * share_rows, share_rows), share_rows)
        size = share_rows // parts
        copies = []
        for part in range(parts):
            copies.append([
                links.push(
                    r.rs_out.at[
                        slot,
                        pl.ds(pl.multiple_of(peer["col"] * share_rows + part * size, size), size),
                    ],
                    r.rs_in.at[slot, me, part * size : part * size + size],
                    peer,
                )
                for peer in peers
            ])
        r.rs_own[slot] = r.part[mine, :]
        return copies

    def tokens_in(slot, copies, part=0, parts=1):
        wait_all(copies[part])
        size = share_rows // parts
        at = slice(part * size, part * size + size)
        total = r.rs_own[slot, at, :]
        for peer in peers:
            total = total + r.rs_in[slot, peer["col"], at, :].astype(F32)
        return total

    def part_rows(part, parts):
        size = share_rows // parts
        return pl.ds(pl.multiple_of(me * share_rows + part * size, size), size)

    own_rows = pl.ds(pl.multiple_of(me * share_rows, share_rows), share_rows)

    def spread_rows(ref, value, part, parts):
        at = part_rows(part, parts)
        ref[at, :] = value
        return to_cols(lambda peer: ref.at[at, :], ref.at[at, :])

    def gain_row(layer):
        return jnp.concatenate([r.gain_all[k, layer : layer + 1, :] for k in range(n)], axis=1)

    def block_of(slot, x_first):
        c, one, two = slot // 4, (slot // 2) % 2, slot % 2
        bx, by = (one, two) if x_first else (two, one)
        return by * 4 + c * 2 + bx

    class Reduce:
        def __init__(self, own, one, kept, two, held, three, x_first):
            self.own, self.one, self.kept = own, one, kept
            self.two, self.held, self.three = two, held, three
            self.at = (x, y) if x_first else (y, x)
            self.to = (over, beside) if x_first else (beside, over)

        def first(self):
            self.copy = links.push(
                self.own.at[pl.ds(pl.multiple_of((1 - core) * 4, 4), 4)], self.one, twin
            )

        def second(self):
            self.copy.wait()
            for j in range(4):
                self.kept[j] = (
                    self.own[core * 4 + j].astype(F32) + self.one[j].astype(F32)
                ).astype(BF)
            self.copy = links.push(
                self.kept.at[pl.ds(pl.multiple_of((1 - self.at[0]) * 2, 2), 2)], self.two, self.to[0]
            )

        def third(self):
            self.copy.wait()
            for j in range(2):
                self.held[j] = (
                    self.kept[self.at[0] * 2 + j].astype(F32) + self.two[j].astype(F32)
                ).astype(BF)
            self.copy = links.push(self.held.at[1 - self.at[1]], self.three, self.to[1])

        def result(self):
            self.copy.wait()
            return self.held[self.at[1]].astype(F32) + self.three[...].astype(F32)

    def reducer(parts, layer, x_first):
        return Reduce(*[part.at[layer] for part in parts], x_first)

    class Total:
        def __init__(self, layer):
            self.layer = layer

        def first(self):
            self.copy = links.push(r.small.at[self.layer, 0], r.small_in.at[self.layer, 0], twin)

        def later(self, stage, peer):
            self.copy.wait()
            r.small[self.layer, stage] = (
                r.small[self.layer, stage - 1] + r.small_in[self.layer, stage - 1]
            )
            self.copy = links.push(
                r.small.at[self.layer, stage], r.small_in.at[self.layer, stage], peer
            )

        def second(self):
            self.later(1, over)

        def third(self):
            self.later(2, beside)

        def result(self):
            self.copy.wait()
            return r.small[self.layer, 2] + r.small_in[self.layer, 2]

    for block in first_in[:3]:
        block.turn()
    wait_all(tok_copies)
    cot_copies = to_cols(lambda at: r.cot, r.cot_all.at[:, lanes(me, width)])
    first = r.tok_all[...].astype(F32)
    first_scale = lax.rsqrt(jnp.sum(first * first, axis=1, keepdims=True) / full + EPSILON)
    r.scale0[...] = first_scale
    r.normed[0] = (first * first_scale * gain_row(0)).astype(BF)
    resid1 = None
    blocks_in, block_out = first_in, first_out
    for layer in range(LAYERS):
        for block in blocks_in[:3]:
            block.end()
        normed = r.normed[layer]
        r.up[layer, 8 : 8 + rows, 0:cols] = mm(normed, r.inner_all[layer])
        r.up[layer, 8 : 8 + rows, cols : cols + state_cols] = mm(normed, r.state_all[layer])
        halo = links.push(r.up.at[layer, rows : rows + 8], r.halo.at[layer], over)
        raw_t = jnp.transpose(mm(normed, r.step_all[layer])) + r.head_par[layer, :, 0:1]
        rate = jnp.exp(r.head_par[layer, :, 1:2])
        step_t = jnp.maximum(raw_t, 0.0) + jnp.log1p(jnp.exp(-jnp.abs(raw_t)))
        decay_t = -rate * step_t
        cum_t = times_selector(decay_t, r.upper[...])
        last = cum_t[:, rows - 1 : rows]
        entry_t = jnp.exp(cum_t) * entry_mask
        tail_t = jnp.exp(last - cum_t) * tail_mask
        r.rows_t[layer, 0] = raw_t
        r.rows_t[layer, 1] = step_t
        r.rows_t[layer, 2] = decay_t
        r.rows_t[layer, 3] = cum_t
        r.passing[layer] = jnp.broadcast_to(jnp.exp(last) * pass_mask, (heads, 128))
        r.columns[layer] = jnp.transpose(jnp.concatenate([step_t, cum_t, entry_t, tail_t], axis=0))
        if layer == 0:
            blocks_in[3].turn()
        halo.wait()
        r.up[layer, 0:8] = r.halo[layer]

        def conv(lo, hi, taps, bias):
            total = jnp.broadcast_to(bias, (rows, hi - lo))
            for k in range(KERNEL):
                term = taps[k : k + 1, :] * r.up[layer, 5 + k : 5 + k + rows, lo:hi]
                total = total + (term if k == KERNEL - 1 else term * same_at(k - 3))
            return total

        pre_q = conv(cols, cols + state_cols, r.pair_taps[layer], r.pair_bias[layer : layer + 1, :])
        pre_u = conv(0, cols, r.taps[layer], r.bias[layer : layer + 1, :])
        r.pre_q[layer] = pre_q
        r.pre_u[layer] = pre_u
        post_q = pre_q * logistic(pre_q)
        post_x = pre_u * logistic(pre_u)
        r.post_q[layer] = post_q
        r.post_x[layer] = post_x
        b_mat, c_mat = post_q[:, :half_state], post_q[:, half_state:]
        columns = r.columns[layer]
        xd = post_x * spread(columns[:, 0:heads])
        r.xd[layer] = xd
        r.fresh[layer] = mm3(xd * spread(columns[:, 3 * heads : 4 * heads]), b_mat, TN)
        r.fresh16[layer] = r.fresh[layer].astype(BF)
        state_copy = links.push(r.fresh16.at[layer], r.entry.at[layer], over)
        c_halves, b_halves = halves(c_mat), halves(b_mat)
        scores = mm_halves(c_halves, b_halves, NT)
        for p in range(pairs):
            xd_halves = halves(r.xd[layer, :, 128 * p : 128 * p + 128])
            outs = []
            for h in (2 * p, 2 * p + 1):
                mixing = jnp.exp(
                    r.columns[layer, :, heads + h : heads + h + 1]
                    - r.rows_t[layer, 3, h : h + 1, :]
                    + r.mask[...]
                )
                outs.append(mm_halves(halves(mixing * scores), xd_halves))
            r.mixed[layer, :, 128 * p : 128 * p + 128] = jnp.where(left, outs[0], outs[1])
        blocks_in[3].end()
        gate_val = mm(normed, r.gate_all[layer])
        r.gate_val[layer] = gate_val
        silu_gate = gate_val * logistic(gate_val)
        state_copy.wait()
        incoming = mm(c_halves[0], r.entry[layer], NT) + mm(c_halves[1], r.entry[layer], NT)
        mixed = r.mixed[layer] + spread(columns[:, 2 * heads : 3 * heads]) * incoming
        r.mixed[layer] = mixed
        gated = (mixed + r.skip_row[layer : layer + 1, :] * post_x) * silu_gate
        r.gated[layer] = gated
        power = row_sums(gated * gated)
        gated_gain = r.gated_gain[layer : layer + 1, :]
        if layer == 0:
            copies = col_exchange(0, power)
            block_out.turn()
            wait_all(cot_copies)
            block_out.end()
            power_sum = col_total(0, copies)[:, 0:1]
        else:
            d_normed_y = mm(r.cot_all[...], r.out_all[layer], NT)
            r.dyn[...] = d_normed_y
            cross = row_sums(d_normed_y * gated_gain * gated)
            keep = lax.broadcasted_iota(jnp.int32, (8, rows), 0) < 1
            copies = col_exchange(1, jnp.where(keep, power, cross))
            sums = col_total(1, copies)
            power_sum = sums[:, 0:1]
            cross_sum = sums[:, 1:2]
        gated_scale = lax.rsqrt(power_sum / (n * cols) + EPSILON)
        r.gated_scale[layer] = gated_scale
        normed_y = (gated * gated_scale * gated_gain).astype(BF)
        r.normed_y[layer] = normed_y
        partial = mm(normed_y, r.out_all[layer])
        if layer == 0:
            turned = tokens_out(0, partial, 2)
            blocks_in = inward(1)
            block_out = outward(1)
            copies = []
            for part in range(2):
                at = slice(part * share_rows // 2, (part + 1) * share_rows // 2)
                resid1 = tokens_in(0, turned, part, 2) + r.tok_all[part_rows(part, 2), :].astype(F32)
                r.resid1[at, :] = resid1
                scale1 = lax.rsqrt(
                    jnp.sum(resid1 * resid1, axis=1, keepdims=True) / full + EPSILON
                )
                r.scale1[at, :] = scale1
                copies += spread_rows(
                    r.normed.at[1], (resid1 * scale1 * gain_row(1)).astype(BF), part, 2
                )
            for block in blocks_in + [block_out]:
                block.turn()
            block_out.end()
            wait_all(copies)
        else:
            turned = tokens_out(1, partial)
    last_out = turned

    def finish_late(at, late):
        r.inner_grad[at] = late[:, 0:cols]
        turned_late = jnp.transpose(late[:, cols : cols + 128])
        r.state_grad[at] = turned_late[0:share, :]
        r.step_grad[at] = turned_late[share : share + heads, :]

    pending = []
    for layer in reversed(range(LAYERS)):
        top = layer == LAYERS - 1
        cot = r.cot_all if top else r.do_all
        gated_gain = r.gated_gain[layer : layer + 1, :]
        gated = r.gated[layer]
        gated_scale = r.gated_scale[layer]
        if top:
            d_normed_y = r.dyn[...]
            scaled_y = d_normed_y * gated_gain
        else:
            d_normed_y = mm(cot[...], r.out_all[layer], NT)
            scaled_y = d_normed_y * gated_gain
            copies = col_exchange(2, row_sums(scaled_y * gated))
        out_grad = reducer(
            (r.out_own, r.out_one, r.out_kept, r.out_two, r.out_held, r.out_three), layer, True
        )
        gate_grad = reducer(
            (r.gate_own, r.gate_one, r.gate_kept, r.gate_two, r.gate_held, r.gate_three), layer, False
        )
        late_grad = reducer(
            (r.late_own, r.late_one, r.late_kept, r.late_two, r.late_held, r.late_three), layer, False
        )
        product = mm(r.normed_y[layer], cot[...], TN)
        for slot in range(8):
            at = 128 * block_of(slot, True)
            r.out_own[layer, slot] = product[:, at : at + 128].astype(BF)
        out_grad.first()
        if not top:
            cross_sum = col_total(2, copies)[:, 0:1]
            lo_copies = to_cols(lambda at: r.lo_out.at[at], r.layer_output.at[own_rows, :])
            grad_copies = to_cols(lambda at: r.grad_out.at[at], r.resid_grad.at[own_rows, :])
            gain_copies = to_cols(lambda at: r.gain_out.at[at], r.gain_in.at[me])
        d_gated = gated_scale * scaled_y - gated * (
            gated_scale * gated_scale * gated_scale * cross_sum / (n * cols)
        )
        gain_y = jnp.sum(d_normed_y * gated * gated_scale, axis=0, keepdims=True)
        gate_val = r.gate_val[layer]
        sigma = logistic(gate_val)
        skip = r.skip_row[layer : layer + 1, :]
        post_x = r.post_x[layer]
        d_mixed = d_gated * (gate_val * sigma)
        r.d_mixed[...] = d_mixed
        columns = r.columns[layer]
        post_q = r.post_q[layer]
        b_mat, c_mat = post_q[:, :half_state], post_q[:, half_state:]
        c_halves, b_halves = halves(c_mat), halves(b_mat)
        reached = halves(spread(columns[:, 2 * heads : 3 * heads]) * d_mixed)
        r.pull_out[layer] = mm_halves(reached, c_halves, TN).astype(BF)
        pull_copy = links.push(r.pull_out.at[layer], r.pull_in.at[layer], over)
        out_grad.second()
        mixed = r.mixed[layer]
        d_gate = (
            d_gated * (mixed + skip * post_x) * sigma * (1.0 + gate_val * (1.0 - sigma))
        ).astype(BF)
        r.d_gate[...] = d_gate
        normed = r.normed[layer]
        product = mm(normed, d_gate, TN)
        for slot in range(8):
            at = 128 * block_of(slot, False)
            r.gate_own[layer, slot] = product[at : at + 128, :].astype(BF)
        gate_grad.first()
        scores_t = mm_halves(b_halves, c_halves, NT)
        for p in range(pairs):
            at = slice(128 * p, 128 * p + 128)
            dy_halves = halves(r.d_mixed[:, at])
            xd_pair = r.xd[layer, :, at]
            outs = []
            for h in (2 * p, 2 * p + 1):
                mixing = jnp.exp(
                    r.rows_t[layer, 3, h : h + 1, :]
                    - r.columns[layer, :, heads + h : heads + h + 1]
                    + r.mask_t[...]
                )
                outs.append(mm_halves(halves(mixing * scores_t), dy_halves))
                chosen = jnp.where(left if h % 2 == 0 else ~left, xd_pair, 0.0)
                crossed = mixing * mm_halves(halves(chosen), dy_halves, NT)
                if h == 0:
                    r.d_scores[...] = crossed
                else:
                    r.d_scores[...] += crossed
            r.d_xd[:, at] = jnp.where(left, outs[0], outs[1])
        d_scores = halves(r.d_scores[...])
        xd = r.xd[layer]
        tail = spread(columns[:, 3 * heads : 4 * heads])
        pull_copy.wait()
        pull = jnp.where(x == 0, r.pull_in[layer].astype(F32), 0.0)
        pull16 = pull.astype(BF)
        entry16 = r.entry[layer]
        entry = entry16.astype(F32)
        tailed = halves(tail * xd)
        d_b = mm_halves(d_scores, c_halves) + (mm(tailed[0], pull16) + mm(tailed[1], pull16))
        d_c = mm_halves(d_scores, b_halves, TN) + (mm(reached[0], entry16) + mm(reached[1], entry16))
        r.share_own[...] = jnp.transpose(jnp.concatenate([d_b, d_c], axis=1))
        r.share_out[layer] = r.share_own[...].astype(BF)
        share_copies = [
            links.push(
                r.share_out.at[
                    layer, pl.ds(pl.multiple_of(peer["col"] * share, share), share)
                ],
                r.share_in.at[layer, me],
                peer,
            )
            for peer in peers
        ]
        d_xd = r.d_xd[...] + tail * (mm(b_halves[0], pull16, NT) + mm(b_halves[1], pull16, NT))
        d_x = spread(columns[:, 0:heads]) * d_xd + skip * d_mixed
        pre_u = r.pre_u[layer]
        sigma = logistic(pre_u)
        d_pre = d_x * sigma * (1.0 + pre_u * (1.0 - sigma))
        r.d_pre[0:rows, :] = d_pre
        r.back_out[layer, :, 0:cols] = d_pre[0:8, :]
        back_copy = links.push(
            r.back_out.at[layer, :, 0:cols], r.back_in.at[layer, :, 0:cols], over
        )
        crossing = per_head(d_mixed * mixed - xd * d_xd)
        moved = per_head(d_xd * post_x)
        skipped = per_head(d_mixed * post_x)
        ended = jnp.sum(
            selector_times(r.pick[...], pull * r.fresh[layer])
            + r.passing[layer] * selector_times(r.pick[...], pull * entry),
            axis=1,
            keepdims=True,
        )
        d_cum = crossing + jnp.where(last_lane, ended, 0.0)
        d_decay = times_selector(d_cum, r.lower[...])
        rate = jnp.exp(r.head_par[layer, :, 1:2])
        d_step = (moved - rate * d_decay) * logistic(r.rows_t[layer, 0])
        d_step16 = jnp.transpose(d_step).astype(BF)
        head_lane = lax.broadcasted_iota(jnp.int32, (heads, 128), 1)
        step_sum = jnp.sum(d_step, axis=1, keepdims=True)
        decay_sum = jnp.sum(d_decay * r.rows_t[layer, 2], axis=1, keepdims=True)
        skip_sum = jnp.sum(skipped, axis=1, keepdims=True)
        head_sums = jnp.where(
            head_lane == 0, step_sum, jnp.where(head_lane == 1, decay_sum, skip_sum)
        )
        gate_grad.second()
        sums = []
        for k in range(KERNEL):
            term = d_pre * r.up[layer, 5 + k : 5 + k + rows, 0:cols]
            term = term if k == KERNEL - 1 else term * same_at(k - 3)
            sums.append(jnp.sum(term, axis=0, keepdims=True))
        sums.append(jnp.sum(d_pre, axis=0, keepdims=True))
        sums.append(gain_y)
        share_pre = own_share(r.pre_q[layer])
        share_taps = own_share(r.pair_taps[layer])
        share_weight = own_share(r.state_all[layer])
        wait_all(share_copies)
        total = r.share_own[pl.ds(pl.multiple_of(me * share, share), share), :]
        for peer in peers:
            total = total + r.share_in[layer, peer["col"]].astype(F32)
        sigma = logistic(share_pre)
        d_share = jnp.transpose(total) * sigma * (1.0 + share_pre * (1.0 - sigma))
        r.d_share[0:rows, :] = d_share
        r.edge_out[layer] = d_share[0:8, :]
        edge_copy = links.push(r.edge_out.at[layer], r.edge_in.at[layer], over)
        out_grad.third()
        r.small[layer, 0, :, 0:cols] = jnp.concatenate(
            sums + [jnp.zeros((2, cols), F32)], axis=0
        )
        state_sums = []
        for k in range(KERNEL):
            term = d_share * own_share(r.up[layer, 5 + k : 5 + k + rows, cols : cols + state_cols])
            term = term if k == KERNEL - 1 else term * same_at(k - 3)
            state_sums.append(jnp.sum(term, axis=0, keepdims=True))
        state_sums.append(jnp.sum(d_share, axis=0, keepdims=True))
        state_sums.append(jnp.zeros((3, share), F32))
        r.small[layer, 0, :, cols : cols + 128] = jnp.concatenate(
            [jnp.concatenate(state_sums, axis=0), jnp.zeros((8, 128 - share), F32)], axis=1
        )
        r.small[layer, 0, :, cols + 128 : cols + 256] = head_sums
        back_copy.wait()
        r.d_pre[rows : rows + 8, :] = r.back_in[layer, :, 0:cols]
        taps = r.taps[layer]
        d_inner = taps[KERNEL - 1 : KERNEL, :] * d_pre
        for lead in range(1, KERNEL):
            k = KERNEL - 1 - lead
            d_inner = d_inner + taps[k : k + 1, :] * r.d_pre[lead : lead + rows, :] * same_at(lead)
        d_inner = d_inner.astype(BF)
        edge_copy.wait()
        r.d_share[rows : rows + 8, :] = r.edge_in[layer]
        d_pair = share_taps[KERNEL - 1 : KERNEL, :] * d_share
        for lead in range(1, KERNEL):
            k = KERNEL - 1 - lead
            d_pair = d_pair + share_taps[k : k + 1, :] * r.d_share[
                lead : lead + rows, :
            ] * same_at(lead)
        d_pair = d_pair.astype(BF)
        misc = jnp.concatenate(
            [
                d_pair.astype(F32),
                d_step16.astype(F32),
                jnp.zeros((rows, 128 - share - heads), F32),
            ],
            axis=1,
        ).astype(BF)
        d_late = jnp.concatenate([d_inner, misc], axis=1)

        def late_product():
            product = mm(normed, d_late, TN)
            for slot in range(8):
                at = 128 * block_of(slot, False)
                r.late_own[layer, slot] = product[at : at + 128, :].astype(BF)
            late_grad.first()

        if not top:
            late_product()
        partial = (
            mm(r.d_gate[...], r.gate_all[layer], NT)
            + mm(d_inner, r.inner_all[layer], NT)
            + mm(d_pair, share_weight, NT)
            + mm(d_step16, r.step_all[layer], NT)
        )
        small = Total(layer)
        if top:
            turned = tokens_out(2, partial, 2)
            gate_grad.third()
            late_product()
            out_rows = (r.resid1[...] + tokens_in(1, last_out)).astype(BF)
            for k in range(n):
                r.lo_out[k] = out_rows[:, k * width : (k + 1) * width]
            r.layer_output[own_rows, :] = r.lo_out[me]
            gain = gain_row(layer)
            copies = []
            gain_sum = jnp.zeros((1, full), F32)
            for part in range(2):
                at = slice(part * share_rows // 2, (part + 1) * share_rows // 2)
                d_normed = tokens_in(2, turned, part, 2)
                resid, scale = r.resid1[at, :], r.scale1[at, :]
                scaled = d_normed * gain
                pulled = jnp.sum(scaled * resid, axis=1, keepdims=True)
                grad = (
                    r.cot_all[part_rows(part, 2), :].astype(F32)
                    + scale * scaled
                    - resid * (scale * scale * scale * pulled / full)
                )
                copies += spread_rows(r.do_all, grad.astype(BF), part, 2)
                gain_sum = gain_sum + jnp.sum(d_normed * resid * scale, axis=0, keepdims=True)
                for k in range(n):
                    r.grad_out[k, at, :] = grad[:, k * width : (k + 1) * width]
            for k in range(n):
                r.gain_out[k] = jnp.broadcast_to(gain_sum[:, k * width : (k + 1) * width], (8, width))
            r.gain_in[me] = r.gain_out[me]
            r.resid_grad[own_rows, :] = r.grad_out[me]
            late_grad.second()
            late_grad.third()
            wait_all(copies)
            pending = [out_grad, gate_grad, late_grad, small]
        else:
            r.part[...] = partial
            for k in range(n):
                r.last_out[k] = partial[:, k * width : (k + 1) * width].astype(BF)
            turned = to_cols(lambda at: r.last_out.at[at], r.last_in.at[me])
            mine = r.part[:, lanes(me, width)]
            gate_grad.third()
            late_grad.second()
            above = layer + 1
            wait_all(gain_copies)
            gain_above = r.gain_in[0]
            for k in range(1, n):
                gain_above = gain_above + r.gain_in[k]
            r.small[above, 0, 6:7, 0:width] = gain_above[0:1, :]
            pending[3].first()
            r.out_grad[above] = pending[0].result()
            r.gate_grad[above] = pending[1].result()
            wait_all(grad_copies)
            wait_all(lo_copies)
            wait_all(turned)
            for peer in peers:
                mine = mine + r.last_in[peer["col"]].astype(F32)
            resid, scale = r.tok_all[:, lanes(me, width)].astype(F32), r.scale0[...]
            scaled = mine * r.gain_all[me, layer : layer + 1, :]
            copies = col_exchange(3, row_sums(scaled * resid))
            r.small[layer, 0, 6:7, 0:width] = jnp.sum(mine * resid * scale, axis=0, keepdims=True)
            small.first()
            late_grad.third()
            pending[3].second()
            finish_late(above, pending[2].result())
            pulled = col_total(3, copies)[:, 0:1]
            r.input_grad[...] = (
                r.resid_grad[...]
                + scale * scaled
                - resid * (scale * scale * scale * pulled / full)
            )
            small.second()
            pending[3].third()
            r.out_grad[layer] = out_grad.result()
            r.gate_grad[layer] = gate_grad.result()
            small.third()
            finish_late(layer, late_grad.result())
            for at, terms in ((above, pending[3]), (layer, small)):
                totals = terms.result()
                r.bias_grad[at : at + 1, :] = totals[4:5, 0:cols]
                r.gained_grad[at : at + 1, :] = totals[5:6, 0:cols]
                r.gain_grad[at : at + 1, :] = totals[6:7, 0:width]
                r.taps_grad[at] = totals[0:KERNEL, 0:cols]
                r.pair_grad[at] = totals[0:KERNEL, cols : cols + share]
                r.pair_bias_grad[at : at + 1, :] = totals[4:5, cols : cols + share]
                of_heads = totals[0:8, cols + 128 : cols + 256]
                r.step_bias_grad[at : at + 1, :] = flat(of_heads[:, 0:1])
                r.decay_grad[at : at + 1, :] = flat(of_heads[:, 1:2])
                r.skip_grad[at : at + 1, :] = flat(of_heads[:, 2:3])


def fused(
    tokens, segment_index, cotangent, norm_gain, gate_weight, inner_weight, state_weight,
    step_weight, inner_kernel, inner_bias, state_kernel, state_bias, step_bias, decay_log,
    skip_gain, gated_gain, output_weight,
):
    n = lax.axis_size("col")
    rows, width = tokens.shape
    full = n * width
    cols, state_cols, heads = inner_kernel.shape[1], state_kernel.shape[1], step_bias.shape[1]
    share = state_cols // n
    share_rows = rows // n
    two = LAYERS
    any_spec = pl.BlockSpec(memory_space=pl.ANY)
    ins = dict(
        tok=tokens,
        in_seg=segment_index,
        cot=cotangent,
        gain=norm_gain,
        in_taps=jnp.swapaxes(inner_kernel, 1, 2),
        in_bias=inner_bias,
        in_gated=gated_gain,
        in_pair_taps=jnp.swapaxes(state_kernel, 1, 2),
        in_pair_bias=state_bias,
        in_step=step_bias,
        in_decay=decay_log,
        in_skip=skip_gain,
        gate=gate_weight,
        inner=inner_weight,
        state=state_weight,
        step=step_weight,
        out=output_weight,
    )
    outs = dict(
        layer_output=((rows, width), BF),
        input_grad=((rows, width), F32),
        gain_grad=((two, width), F32),
        gate_grad=((two, full // 8, cols), F32),
        inner_grad=((two, full // 8, cols), F32),
        state_grad=((two, share, full // 8), F32),
        step_grad=((two, heads, full // 8), F32),
        taps_grad=((two, KERNEL, cols), F32),
        bias_grad=((two, cols), F32),
        pair_grad=((two, KERNEL, share), F32),
        pair_bias_grad=((two, share), F32),
        step_bias_grad=((two, heads), F32),
        decay_grad=((two, heads), F32),
        skip_grad=((two, heads), F32),
        gained_grad=((two, cols), F32),
        out_grad=((two, cols, full // 8), F32),
    )
    scratch = dict(
        seg=((1, 2 * rows), jnp.int32),
        taps=((two, KERNEL, cols), F32),
        bias=((two, cols), F32),
        gated_gain=((two, cols), F32),
        pair_taps=((two, KERNEL, state_cols), F32),
        pair_bias=((two, state_cols), F32),
        step_bias=((two, heads), F32),
        decay_log=((two, heads), F32),
        skip_gain=((two, heads), F32),
        head_par=((two, heads, 128), F32),
        skip_row=((two, cols), F32),
        fresh16=((two, cols, state_cols // 2), BF),
        share_own=((state_cols, rows), F32),
        tok_all=((rows, full), BF),
        cot_all=((rows, full), BF),
        do_all=((rows, full), BF),
        gain_all=((n, two, width), F32),
        gate_all=((two, full, cols), BF),
        inner_all=((two, full, cols), BF),
        state_all=((two, full, state_cols), BF),
        step_all=((two, full, heads), BF),
        out_all=((two, cols, full), BF),
        segp=((2 * rows + 16, 8), F32),
        mask=((rows, rows), F32),
        mask_t=((rows, rows), F32),
        upper=((rows, rows), BF),
        lower=((rows, rows), BF),
        pick=((heads, cols), BF),
        scale0=((rows, 1), F32),
        scale1=((share_rows, 1), F32),
        resid1=((share_rows, full), F32),
        normed=((two, rows, full), BF),
        up=((two, rows + 8, cols + state_cols), F32),
        halo=((two, 8, cols + state_cols), F32),
        rows_t=((two, 4, heads, rows), F32),
        passing=((two, heads, 128), F32),
        columns=((two, rows, 4 * heads), F32),
        gate_val=((two, rows, cols), F32),
        pre_u=((two, rows, cols), F32),
        pre_q=((two, rows, state_cols), F32),
        post_x=((two, rows, cols), F32),
        post_q=((two, rows, state_cols), F32),
        xd=((two, rows, cols), F32),
        fresh=((two, cols, state_cols // 2), F32),
        entry=((two, cols, state_cols // 2), BF),
        mixed=((two, rows, cols), F32),
        gated=((two, rows, cols), F32),
        gated_scale=((two, rows, 1), F32),
        normed_y=((two, rows, cols), BF),
        dyn=((rows, cols), F32),
        part=((rows, full), F32),
        rs_out=((3, rows, full), BF),
        rs_in=((3, n, share_rows, full), BF),
        rs_own=((3, share_rows, full), F32),
        sum_own=((4, 8, rows), F32),
        sum_all=((4, n, 8, rows), F32),
        d_mixed=((rows, cols), F32),
        d_gate=((rows, cols), BF),
        d_scores=((rows, rows), F32),
        d_xd=((rows, cols), F32),
        pull_out=((two, cols, state_cols // 2), BF),
        pull_in=((two, cols, state_cols // 2), BF),
        share_out=((two, state_cols, rows), BF),
        share_in=((two, n, share, rows), BF),
        d_pre=((rows + 8, cols), F32),
        back_out=((two, 8, cols), F32),
        back_in=((two, 8, cols), F32),
        d_share=((rows + 8, share), F32),
        edge_out=((two, 8, share), F32),
        edge_in=((two, 8, share), F32),
        small=((two, 3, 8, cols + 256), F32),
        small_in=((two, 3, 8, cols + 256), F32),
        lo_out=((n, share_rows, width), BF),
        grad_out=((n, share_rows, width), F32),
        resid_grad=((rows, width), F32),
        gain_out=((n, 8, width), F32),
        gain_in=((n, 8, width), F32),
        last_out=((n, rows, width), BF),
        last_in=((n, rows, width), BF),
    )
    deep = full // 8

    def stages(shape):
        return [((two,) + count + shape, BF) for count in ((8,), (4,), (4,), (2,), (2,), ())]

    o = stages((cols, deep))
    g = stages((deep, cols))
    t = stages((deep, cols + 128))
    scratch.update(
        out_own=o[0], out_one=o[1], out_kept=o[2], out_two=o[3], out_held=o[4], out_three=o[5],
        gate_own=g[0], gate_one=g[1], gate_kept=g[2], gate_two=g[3], gate_held=g[4],
        gate_three=g[5], late_own=t[0], late_one=t[1], late_kept=t[2], late_two=t[3],
        late_held=t[4], late_three=t[5],
    )
    copies = 192
    scratch.update(
        send=copies, recv=copies, here=32,
    )
    results = pl.pallas_call(
        functools.partial(fused_kernel, n, list(ins) + list(outs) + list(scratch)),
        out_shape=[jax.ShapeDtypeStruct(*one) for one in outs.values()],
        in_specs=[any_spec] * len(ins),
        out_specs=[VMEM_SPEC] * len(outs),
        scratch_shapes=[
            pltpu.SemaphoreType.DMA((one,)) if isinstance(one, int) else pltpu.VMEM(*one)
            for one in scratch.values()
        ],
        compiler_params=pltpu.CompilerParams(
            collective_id=9, has_side_effects=True, vmem_limit_bytes=60 * 2**20
        ),
        name="fused",
    )(*ins.values())
    results = list(
        pl.pallas_call(
            hand_over,
            out_shape=[jax.ShapeDtypeStruct(*one) for one in outs.values()],
            in_specs=[VMEM_SPEC] * len(outs),
            out_specs=[any_spec] * len(outs),
            scratch_shapes=[pltpu.SemaphoreType.DMA((len(outs),))],
            name="hand_over",
        )(*results)
    )
    for at in (5, 6, 7, 9):
        results[at] = jnp.swapaxes(results[at], 1, 2)
    return tuple(results)


def hand_over(*refs):
    sems = refs[-1]
    count = (len(refs) - 1) // 2
    copies = []
    for at in range(count):
        copy = pltpu.make_async_copy(refs[at], refs[count + at], sems.at[at])
        copy.start()
        copies.append(copy)
    for copy in copies:
        copy.wait()


def solution(mesh):
    placed = (
        P(("dp", "row"), "col"),
        P("dp", None),
        P(("dp", "row"), "col"),
        P(None, "col"),
        P(None, "row", "col"),
        P(None, "row", "col"),
        P(None, "row", None),
        P(None, "row", "col"),
        P(None, "col", None),
        P(None, "col"),
        P(),
        P(),
        P(None, "col"),
        P(None, "col"),
        P(None, "col"),
        P(None, "col"),
        P(None, "col", "row"),
    )
    def run(*args):
        whole = (
            lax.axis_size("row") == 2
            and lax.axis_size("dp") == 4
            and lax.axis_size("col") == 4
            and args[0].shape[0] == SPAN
            and args[7].shape[2] == 8
            and args[3].shape[1] * lax.axis_size("col") == 1024
        )
        return fused(*args) if whole else local(*args)

    return jax.shard_map(
        run,
        mesh=mesh,
        in_specs=placed,
        out_specs=(
            P(("dp", "row"), "col"),
            P(("dp", "row"), "col"),
            P(None, "col"),
            P(None, ("dp", "row"), "col"),
            P(None, ("dp", "row"), "col"),
            P(None, ("dp", "row"), "col"),
            P(None, ("dp", "row"), "col"),
            P(None, "col", None),
            P(None, "col"),
            P(None, "col", None),
            P(None, "col"),
            P(None, "col"),
            P(None, "col"),
            P(None, "col"),
            P(None, "col"),
            P(None, "col", ("dp", "row")),
        ),
        check_vma=False,
    )
```
